256 devices in a mesh: gx: 32 (over y, x, core), gy: 8 (over z).
Axes of the slice: x: 4, y: 4, z: 8, core: 2. Of those that a mesh axis runs over, the one named last changes fastest.
Arguments:
- velocity: float32 [2, 3, 1536, 1024], P(None, None, 'gx', 'gy'), may hold values from -6 to 6
- stretch: float32 [1024], replicated, may hold values from 0.7 to 1.4
- second_metric: float32 [1024], replicated, may hold values from -1 to 1
Outputs:
- section_rhs: float32 [2, 3, 1536, 1024], P(None, None, 'gx', 'gy')
The draws below stay inside these ranges and needn't reach their ends.
All inputs are finite; a program needn't handle non-finite values.
Results may differ from the reference program's by a relative error of at most 0.000054.
Values sent between devices are 32-bit elements; how exact they have to be, the bound alone decides.
A program may use at most 64 MiB of HBM per device.

```python
import math
import jax
import jax.numpy as jnp
from jax import lax

SZ = 2
NX = 1536
NY = 1024


def levels(rng, extent, pieces, low, high):
    loudness = 1.0
    for axis_at, blocks in pieces:
        steps = jax.random.uniform(jax.random.fold_in(jax.random.fold_in(rng, 6), axis_at), (blocks,), jnp.float32, low / len(pieces), high / len(pieces))
        loudness = loudness * jnp.repeat(jnp.exp(steps), extent[axis_at] // blocks).reshape((-1,) + (1,) * (len(extent) - 1 - axis_at))
    return loudness


def noise(rng, dims, deviation, limit, pieces=(), kind=jnp.bfloat16):
    drawn = jax.random.normal(rng, dims, jnp.float32) * deviation
    if len(pieces) > 0:
        drawn = levels(rng, dims, pieces, -0.22, 0.18) * drawn
    return jnp.clip(drawn, min=-limit, max=limit).astype(kind)


def setup_inputs(seed: int = 0) -> dict:
    streams_of = jax.random.split(jax.random.key(seed), 4)
    return {
        "velocity": noise(streams_of[0], (SZ, 3, NX, NY), 1.0, 6.0, ((2, 32), (3, 8)), jnp.float32),
        "stretch": jnp.clip(jnp.exp(jax.random.uniform(streams_of[1], (NY,), jnp.float32, math.log(0.7), math.log(1.4))), 0.7, 1.4),
        "second_metric": jnp.clip(jax.random.uniform(streams_of[2], (NY,), jnp.float32, -1.0, 1.0), -1.0, 1.0),
    }


VISCOSITY = 0.5

def x_stencils(padded, length):
    axis_pos = padded.ndim - 2
    centre = lax.slice_in_dim(padded, 2, 2 + length, axis=axis_pos)
    plus_one = lax.slice_in_dim(padded, 3, 3 + length, axis=axis_pos)
    minus_one = lax.slice_in_dim(padded, 1, 1 + length, axis=axis_pos)
    plus_two = lax.slice_in_dim(padded, 4, 4 + length, axis=axis_pos)
    minus_two = lax.slice_in_dim(padded, 0, length, axis=axis_pos)
    first_rhs = 7.0 / 9.0 * (plus_one - minus_one) + 1.0 / 36.0 * (plus_two - minus_two)
    second = 12.0 / 11.0 * (plus_one - 2.0 * centre + minus_one) + 3.0 / 44.0 * (plus_two - 2.0 * centre + minus_two)
    return (first_rhs, second)

def y_stencils(padded, local, row_ids, total_rows):
    length = local.shape[-1]
    centre = padded[..., 2:2 + length]
    plus_one = padded[..., 3:3 + length]
    minus_one = padded[..., 1:1 + length]
    plus_two = padded[..., 4:4 + length]
    minus_two = padded[..., 0:length]
    near_wall = (row_ids == 1) | (row_ids == total_rows - 2)
    start_edge = row_ids == 0
    end_edge = row_ids == total_rows - 1
    head_rows = local[..., 0:4]
    tail_rows = local[..., length - 4:length]
    first_start = (-3.0 * head_rows[..., 0:1] + 4.0 * head_rows[..., 1:2] - head_rows[..., 2:3]) / 2.0
    first_end = (3.0 * tail_rows[..., 3:4] - 4.0 * tail_rows[..., 2:3] + tail_rows[..., 1:2]) / 2.0
    second_start = 2.0 * head_rows[..., 0:1] - 5.0 * head_rows[..., 1:2] + 4.0 * head_rows[..., 2:3] - head_rows[..., 3:4]
    second_end = 2.0 * tail_rows[..., 3:4] - 5.0 * tail_rows[..., 2:3] + 4.0 * tail_rows[..., 1:2] - tail_rows[..., 0:1]
    inner_first = 7.0 / 9.0 * (plus_one - minus_one) + 1.0 / 36.0 * (plus_two - minus_two)
    inner_second = 12.0 / 11.0 * (plus_one - 2.0 * centre + minus_one) + 3.0 / 44.0 * (plus_two - 2.0 * centre + minus_two)
    first_rhs = jnp.where(near_wall, 0.75 * (plus_one - minus_one), inner_first)
    first_rhs = jnp.where(start_edge, first_start, jnp.where(end_edge, first_end, first_rhs))
    second = jnp.where(near_wall, 1.2 * (plus_one - 2.0 * centre + minus_one), inner_second)
    second = jnp.where(start_edge, second_start, jnp.where(end_edge, second_end, second))
    return (first_rhs, second)

def y_coefs(row_ids, total_rows):
    near_wall = (row_ids == 1) | (row_ids == total_rows - 2)
    edge_rows = (row_ids == 0) | (row_ids == total_rows - 1)
    band_one = jnp.where(edge_rows, 0.0, jnp.where(near_wall, 0.25, 1.0 / 3.0))
    band_two = jnp.where(edge_rows, 0.0, jnp.where(near_wall, 0.1, 2.0 / 11.0))
    return (band_one, band_two)

def cyclic_solve(right_side, coefficient):
    length = right_side.shape[-2]
    moved = jnp.moveaxis(right_side, -2, 0)
    moved_shape = moved.shape
    columns = moved.reshape(length, -1)
    indices = jnp.arange(length)
    side_band = jnp.full((length,), coefficient, dtype=right_side.dtype)
    lower_band = jnp.where(indices == 0, 0.0, side_band).astype(right_side.dtype)
    upper_band = jnp.where(indices == length - 1, 0.0, side_band).astype(right_side.dtype)
    centre_band = jnp.where(indices == 0, 2.0, jnp.where(indices == length - 1, 1.0 + coefficient * coefficient, 1.0)).astype(right_side.dtype)
    column = jnp.where(indices == 0, -1.0, jnp.where(indices == length - 1, coefficient, 0.0)).astype(right_side.dtype)
    stacked = jnp.concatenate([columns, column[:, None]], axis=1)
    solved = lax.linalg.tridiagonal_solve(lower_band, centre_band, upper_band, stacked)
    base_part = solved[:, :-1]
    spread = solved[:, -1]
    factor = (base_part[0] - coefficient * base_part[-1]) / (1.0 + spread[0] - coefficient * spread[-1])
    result = base_part - spread[:, None] * factor[None, :]
    return jnp.moveaxis(result.reshape(moved_shape), 0, -2)

def band_solve(right_side, band_coef):
    length = right_side.shape[-1]
    moved = jnp.moveaxis(right_side, -1, 0)
    moved_shape = moved.shape
    columns = moved.reshape(length, -1)
    band_coef = band_coef.astype(right_side.dtype)
    diagonal = jnp.ones((length,), right_side.dtype)
    solved = lax.linalg.tridiagonal_solve(band_coef, diagonal, band_coef, columns)
    return jnp.moveaxis(solved.reshape(moved_shape), 0, -1)

def plane_terms(velocity_plane, stretch, second_metric):
    padded_x = jnp.concatenate([velocity_plane[:, -2:, :], velocity_plane, velocity_plane[:, :2, :]], axis=1)
    first_x, second_x = x_stencils(padded_x, NX)
    grad_x = cyclic_solve(first_x, 1.0 / 3.0)
    curv_x = cyclic_solve(second_x, 2.0 / 11.0)
    padded_y = jnp.pad(velocity_plane, ((0, 0), (0, 0), (2, 2)))
    row_ids = jnp.arange(NY)
    first_y, second_y = y_stencils(padded_y, velocity_plane, row_ids, NY)
    band_one, band_two = y_coefs(row_ids, NY)
    eta_one = band_solve(first_y, band_one)
    eta_two = band_solve(second_y, band_two)
    grad_y = eta_one / stretch
    curv_y = eta_two / (stretch * stretch) - second_metric * eta_one / (stretch * stretch * stretch)
    return -(velocity_plane[0:1] * grad_x + velocity_plane[1:2] * grad_y) + VISCOSITY * (curv_x + curv_y)

def reference(velocity, stretch, second_metric):
    return lax.map(lambda plane_vel: plane_terms(plane_vel, stretch, second_metric), velocity)
```

```python
import functools

import jax
import jax.numpy as jnp
import numpy as np
from jax import lax
from jax.experimental import pallas as pl
from jax.experimental.pallas import tpu as pltpu
from jax.sharding import PartitionSpec as P

MESH = pl.DeviceIdType.MESH
HIGHEST = lax.Precision.HIGHEST

C1, C2 = 1.0 / 3.0, 2.0 / 11.0
R1 = (-1.0 + np.sqrt(1.0 - 4.0 * C1 * C1)) / (2.0 * C1)
R2 = (-1.0 + np.sqrt(1.0 - 4.0 * C2 * C2)) / (2.0 * C2)
K1 = 1.0 / (1.0 + 2.0 * C1 * R1)
K2 = 1.0 / (1.0 + 2.0 * C2 * R2)
G1 = (25.0 / 36.0) * K1 * (R1 - 1.0 / R1)
G2 = -(75.0 / 88.0) * 7.5 * K2
NEAR1 = -1.0 / 12.0
NEAR2 = 3.0 / 8.0
ZERO2 = (75.0 / 88.0) * (5.5 - 7.5 * K2) - 0.75


def x_tables(rows):
    d = np.arange(rows)[:, None] - np.arange(rows)[None, :]
    first = G1 * np.sign(d) * R1 ** np.abs(d) + NEAR1 * np.where(np.abs(d) == 1, np.sign(d), 0)
    second = G2 * R2 ** np.abs(d) * (d != 0) + NEAR2 * (np.abs(d) == 1) + ZERO2 * (d == 0)
    inner = np.concatenate([first, 0.5 * second])
    up = np.arange(1, rows + 1)
    down = rows - np.arange(rows)
    powers = np.stack([R1**up, R1**down, R2**up, R2**down])
    powers = np.broadcast_to(powers[:, :, None], (4, rows, 128))
    return inner.astype(np.float32), powers.astype(np.float32)


def y_tables(total, width):
    rows = np.arange(total)
    near = (rows == 1) | (rows == total - 2)
    edge = (rows == 0) | (rows == total - 1)
    bands = (
        np.where(edge, 0.0, np.where(near, 0.25, C1)),
        np.where(edge, 0.0, np.where(near, 0.1, C2)),
    )
    b1 = np.zeros((total, total))
    b2 = np.zeros((total, total))
    for j in range(2, total - 2):
        b1[j, j - 2 : j + 3] = [-1 / 36, -7 / 9, 0.0, 7 / 9, 1 / 36]
        b2[j, j - 2 : j + 3] = [3 / 44, 12 / 11, -24 / 11 - 6 / 44, 12 / 11, 3 / 44]
    for j in (1, total - 2):
        b1[j, j - 1 : j + 2] = [-0.75, 0.0, 0.75]
        b2[j, j - 1 : j + 2] = [1.2, -2.4, 1.2]
    b1[0, :3] = [-1.5, 2.0, -0.5]
    b1[-1, -3:] = [0.5, -2.0, 1.5]
    b2[0, :4] = [2.0, -5.0, 4.0, -1.0]
    b2[-1, -4:] = [-1.0, 4.0, -5.0, 2.0]
    whole = []
    for band, b in zip(bands, (b1, b2)):
        a = np.eye(total) + np.diag(band[1:], -1) + np.diag(band[:-1], 1)
        whole.append(np.linalg.solve(a, b))
    blocks = total // width
    inner = np.zeros((blocks, width, 2 * width))
    for q in range(blocks):
        own = slice(q * width, (q + 1) * width)
        inner[q, :, :width] = whole[0][own, own].T
        inner[q, :, width:] = 0.5 * whole[1][own, own].T
    up = np.arange(1, width + 1)
    down = width - np.arange(width)
    gather = np.zeros((8, width))
    gather[0], gather[1], gather[2, -1] = R1**down, R2**down, 1.0
    gather[3], gather[4], gather[5, 0] = R1**up, R2**up, 1.0
    spread = np.zeros((16, 2 * width))
    spread[0, :width] = G1 * R1 ** (up - 1)
    spread[1, width:] = 0.5 * G2 * R2 ** (up - 1)
    spread[2, 0], spread[2, width] = NEAR1, 0.5 * NEAR2
    spread[11, :width] = -G1 * R1 ** (down - 1)
    spread[12, width:] = 0.5 * G2 * R2 ** (down - 1)
    spread[13, width - 1], spread[13, 2 * width - 1] = -NEAR1, 0.5 * NEAR2
    small = np.finfo(np.float32).tiny
    return [
        np.where(np.abs(t) < small, 0.0, t).astype(np.float32)
        for t in (inner, gather, spread)
    ]


def kernel(
    nx, ny, vel, powers, x_inner, y_inner, gather, spread, stretch, metric, out,
    f, pw, wx, wy, ga, sp, st, sm, z, xs, ys, xr, xf, yr,
    load_sem, store_sem, send_sem, recv_sem,
):
    gx = lax.axis_index("gx")
    gy = lax.axis_index("gy")
    rows = f.shape[1]
    width = f.shape[2]
    comps = f.shape[0]

    loads = [
        pltpu.make_async_copy(src, dst, load_sem.at[n])
        for n, (src, dst) in enumerate(
            (
                (vel, f), (powers, pw), (gather, ga), (x_inner, wx),
                (y_inner.at[gy], wy), (spread, sp), (stretch, st), (metric, sm),
            )
        )
    ]
    for copy in loads:
        copy.start()

    right, left = lax.rem(gx + 1, nx), lax.rem(gx + nx - 1, nx)
    right2, left2 = lax.rem(gx + 2, nx), lax.rem(gx + nx - 2, nx)
    barrier = pltpu.get_barrier_semaphore()
    for peer in (right, left, right2, left2):
        pl.semaphore_signal(barrier, inc=1, device_id=(peer, gy), device_id_type=MESH)

    @pl.when(gy > 0)
    def _():
        pl.semaphore_signal(barrier, inc=1, device_id=(gx, gy - 1), device_id_type=MESH)

    @pl.when(gy < ny - 1)
    def _():
        pl.semaphore_signal(barrier, inc=1, device_id=(gx, gy + 1), device_id_type=MESH)

    for copy in loads[:2]:
        copy.wait()
    for c in range(comps):
        fc = f[c]
        xs[0, c : c + 1] = jnp.sum(fc * pw[1], axis=0, keepdims=True)
        xs[0, 8 + c : 9 + c] = jnp.sum(fc * pw[3], axis=0, keepdims=True)
        xs[0, 16 + c : 17 + c] = fc[rows - 1 : rows]
        xs[1, c : c + 1] = jnp.sum(fc * pw[0], axis=0, keepdims=True)
        xs[1, 8 + c : 9 + c] = jnp.sum(fc * pw[2], axis=0, keepdims=True)
        xs[1, 16 + c : 17 + c] = fc[0:1]

    beside_y = jnp.minimum(gy, 1) + jnp.minimum(ny - 1 - gy, 1)
    pl.semaphore_wait(barrier, 4 + beside_y)

    def send(n, src, dst, peer):
        return pltpu.make_async_remote_copy(
            src_ref=src, dst_ref=dst, send_sem=send_sem.at[n], recv_sem=recv_sem.at[n],
            device_id=peer, device_id_type=MESH,
        )

    x_copies = [
        send(0, xs.at[0], xr.at[0], (right, gy)),
        send(1, xs.at[1], xr.at[1], (left, gy)),
        send(2, xs.at[0, 0:16], xf.at[0], (right2, gy)),
        send(3, xs.at[1, 0:16], xf.at[1], (left2, gy)),
    ]
    for copy in x_copies:
        copy.start()

    loads[2].wait()
    flat = f[...].reshape(comps * rows, width)
    ys[...] = lax.dot_general(
        ga[...], flat, (((1,), (1,)), ((), ())), precision=HIGHEST,
        preferred_element_type=jnp.float32,
    )
    y_right = send(4, ys, yr.at[0:8], (gx, gy + 1))
    y_left = send(5, ys, yr.at[8:16], (gx, gy - 1))

    @pl.when(gy < ny - 1)
    def _():
        y_right.start()

    @pl.when(gy > 0)
    def _():
        y_left.start()

    @pl.when(gy == 0)
    def _():
        yr[0:8] = jnp.zeros((8, comps * rows), jnp.float32)

    @pl.when(gy == ny - 1)
    def _():
        yr[8:16] = jnp.zeros((8, comps * rows), jnp.float32)

    for copy in loads[3:]:
        copy.wait()
    side = jnp.concatenate([f[c] for c in range(comps)], axis=1)
    own_x = jnp.dot(wx[...], side, precision=HIGHEST, preferred_element_type=jnp.float32)
    own_y = jnp.dot(flat, wy[...], precision=HIGHEST, preferred_element_type=jnp.float32)
    inv = 1.0 / st[pl.ds(gy, 1), :]
    inv2 = inv * inv
    bend = -0.5 * sm[pl.ds(gy, 1), :] * inv2 * inv

    def along_y(part, c):
        block = part[c * rows : (c + 1) * rows]
        v = f[3 * (c // 3) + 1]
        return block[:, :width] * (bend - v * inv) + block[:, width:] * inv2

    for c in range(comps):
        lanes = slice(c * width, (c + 1) * width)
        u = f[3 * (c // 3)]
        z[c] = own_x[rows:, lanes] - u * own_x[:rows, lanes] + along_y(own_y, c)

    for copy in x_copies:
        copy.wait_recv()
    far1 = np.float32(R1**rows)
    far2 = np.float32(R2**rows)
    left1 = (xr[0, 0:8] + far1 * xf[0, 0:8]) * np.float32(G1 / R1)
    left2_ = (xr[0, 8:16] + far2 * xf[0, 8:16]) * np.float32(0.5 * G2 / R2)
    right1 = (xr[1, 0:8] + far1 * xf[1, 0:8]) * np.float32(-G1 / R1)
    right2_ = (xr[1, 8:16] + far2 * xf[1, 8:16]) * np.float32(0.5 * G2 / R2)
    for c in range(comps):
        row = slice(c, c + 1)
        u = f[3 * (c // 3)]
        first = pw[0] * left1[row] + pw[1] * right1[row]
        second = pw[2] * left2_[row] + pw[3] * right2_[row]
        z[c] = z[c] + (second - u * first)
        near = 0.5 * NEAR2 - NEAR1 * u[0:1]
        z[c, 0:1] = z[c, 0:1] + near * xr[0, 16 + c : 17 + c]
        near = 0.5 * NEAR2 + NEAR1 * u[rows - 1 : rows]
        z[c, rows - 1 : rows] = z[c, rows - 1 : rows] + near * xr[1, 16 + c : 17 + c]

    @pl.when(gy > 0)
    def _():
        y_right.wait_recv()

    @pl.when(gy < ny - 1)
    def _():
        y_left.wait_recv()

    beside = lax.dot_general(
        yr[...], sp[...], (((0,), (0,)), ((), ())), precision=HIGHEST,
        preferred_element_type=jnp.float32,
    )
    stores = []
    for c in range(comps):
        z[c] = z[c] + along_y(beside, c)
        stores.append(pltpu.make_async_copy(z.at[c], out.at[c], store_sem.at[c]))
        stores[-1].start()

    for copy in x_copies:
        copy.wait_send()

    @pl.when(gy < ny - 1)
    def _():
        y_right.wait_send()

    @pl.when(gy > 0)
    def _():
        y_left.wait_send()

    for copy in stores:
        copy.wait()


def solution(mesh):
    nx, ny = mesh.shape["gx"], mesh.shape["gy"]

    def shards(velocity, stretch, second_metric):
        planes, parts, rows, width = velocity.shape
        comps = planes * parts
        x_inner, powers = x_tables(rows)
        y_inner, gather, spread = y_tables(ny * width, width)
        hbm = pl.BlockSpec(memory_space=pltpu.MemorySpace.HBM)
        f32 = jnp.float32
        out = pl.pallas_call(
            functools.partial(kernel, nx, ny),
            out_shape=jax.ShapeDtypeStruct((comps, rows, width), f32),
            in_specs=[hbm] * 8,
            out_specs=hbm,
            scratch_shapes=[
                pltpu.VMEM((comps, rows, width), f32),
                pltpu.VMEM((4, rows, 128), f32),
                pltpu.VMEM((2 * rows, rows), f32),
                pltpu.VMEM((width, 2 * width), f32),
                pltpu.VMEM((8, width), f32),
                pltpu.VMEM((16, 2 * width), f32),
                pltpu.VMEM((ny, width), f32),
                pltpu.VMEM((ny, width), f32),
                pltpu.VMEM((comps, rows, width), f32),
                pltpu.VMEM((2, 24, width), f32),
                pltpu.VMEM((8, comps * rows), f32),
                pltpu.VMEM((2, 24, width), f32),
                pltpu.VMEM((2, 16, width), f32),
                pltpu.VMEM((16, comps * rows), f32),
                pltpu.SemaphoreType.DMA((8,)),
                pltpu.SemaphoreType.DMA((comps,)),
                pltpu.SemaphoreType.DMA((6,)),
                pltpu.SemaphoreType.DMA((6,)),
            ],
            compiler_params=pltpu.CompilerParams(collective_id=0, has_side_effects=True),
        )(
            velocity.reshape(comps, rows, width),
            jnp.asarray(powers), jnp.asarray(x_inner), jnp.asarray(y_inner),
            jnp.asarray(gather), jnp.asarray(spread),
            stretch.reshape(ny, width), second_metric.reshape(ny, width),
        )
        return out.reshape(velocity.shape)

    return jax.shard_map(
        shards,
        mesh=mesh,
        in_specs=(P(None, None, "gx", "gy"), P(), P()),
        out_specs=P(None, None, "gx", "gy"),
        check_vma=False,
    )
```

```python
import functools

import jax
import jax.numpy as jnp
import numpy as np
from jax import lax
from jax.experimental import pallas as pl
from jax.experimental.pallas import tpu as pltpu
from jax.sharding import PartitionSpec as P

MESH = pl.DeviceIdType.MESH
HIGHEST = lax.Precision.HIGHEST

C1, C2 = 1.0 / 3.0, 2.0 / 11.0
R1 = (-1.0 + np.sqrt(1.0 - 4.0 * C1 * C1)) / (2.0 * C1)
R2 = (-1.0 + np.sqrt(1.0 - 4.0 * C2 * C2)) / (2.0 * C2)
K1 = 1.0 / (1.0 + 2.0 * C1 * R1)
K2 = 1.0 / (1.0 + 2.0 * C2 * R2)
G1 = (25.0 / 36.0) * K1 * (R1 - 1.0 / R1)
G2 = -(75.0 / 88.0) * 7.5 * K2
NEAR1 = -1.0 / 12.0
NEAR2 = 3.0 / 8.0
ZERO2 = (75.0 / 88.0) * (5.5 - 7.5 * K2) - 0.75


def x_tables(rows):
    d = np.arange(rows)[:, None] - np.arange(rows)[None, :]
    first = G1 * np.sign(d) * R1 ** np.abs(d) + NEAR1 * np.where(np.abs(d) == 1, np.sign(d), 0)
    second = G2 * R2 ** np.abs(d) * (d != 0) + NEAR2 * (np.abs(d) == 1) + ZERO2 * (d == 0)
    inner = np.concatenate([first, 0.5 * second])
    return inner.astype(np.float32)


def y_tables(total, width):
    rows = np.arange(total)
    near = (rows == 1) | (rows == total - 2)
    edge = (rows == 0) | (rows == total - 1)
    bands = (
        np.where(edge, 0.0, np.where(near, 0.25, C1)),
        np.where(edge, 0.0, np.where(near, 0.1, C2)),
    )
    b1 = np.zeros((total, total))
    b2 = np.zeros((total, total))
    for j in range(2, total - 2):
        b1[j, j - 2 : j + 3] = [-1 / 36, -7 / 9, 0.0, 7 / 9, 1 / 36]
        b2[j, j - 2 : j + 3] = [3 / 44, 12 / 11, -24 / 11 - 6 / 44, 12 / 11, 3 / 44]
    for j in (1, total - 2):
        b1[j, j - 1 : j + 2] = [-0.75, 0.0, 0.75]
        b2[j, j - 1 : j + 2] = [1.2, -2.4, 1.2]
    b1[0, :3] = [-1.5, 2.0, -0.5]
    b1[-1, -3:] = [0.5, -2.0, 1.5]
    b2[0, :4] = [2.0, -5.0, 4.0, -1.0]
    b2[-1, -4:] = [-1.0, 4.0, -5.0, 2.0]
    whole = []
    for band, b in zip(bands, (b1, b2)):
        a = np.eye(total) + np.diag(band[1:], -1) + np.diag(band[:-1], 1)
        whole.append(np.linalg.solve(a, b))
    blocks = total // width
    inner = np.zeros((blocks, width, 2 * width))
    for q in range(blocks):
        own = slice(q * width, (q + 1) * width)
        inner[q, :, :width] = whole[0][own, own].T
        inner[q, :, width:] = 0.5 * whole[1][own, own].T
    up = np.arange(1, width + 1)
    down = width - np.arange(width)
    gather = np.zeros((8, width))
    gather[0], gather[1], gather[2, -1] = R1**down, R2**down, 1.0
    gather[3], gather[4], gather[5, 0] = R1**up, R2**up, 1.0
    spread = np.zeros((16, 2 * width))
    spread[0, :width] = G1 * R1 ** (up - 1)
    spread[1, width:] = 0.5 * G2 * R2 ** (up - 1)
    spread[2, 0], spread[2, width] = NEAR1, 0.5 * NEAR2
    spread[11, :width] = -G1 * R1 ** (down - 1)
    spread[12, width:] = 0.5 * G2 * R2 ** (down - 1)
    spread[13, width - 1], spread[13, 2 * width - 1] = -NEAR1, 0.5 * NEAR2
    small = np.finfo(np.float32).tiny
    return [
        np.where(np.abs(t) < small, 0.0, t).astype(np.float32)
        for t in (inner, gather, spread)
    ]


FAR = True


def kernel(
    nx, ny, vel, tables, stretch, metric, out, f, late, xs, ys, xr, yr,
    load_sem, x_sem, y_sem,
):
    gx = lax.axis_index("gx")
    gy = lax.axis_index("gy")
    comps, rows, width = f.shape
    steps = rows // 8
    t_rows = tables.shape[1]

    def row_copy(n):
        part = slice(n * comps // 3, (n + 1) * comps // 3)
        return pltpu.make_async_copy(vel.at[part], f.at[part], load_sem.at[0])

    for n in range(3):
        row_copy(n).start()

    odd = lax.rem(gx, 2)
    side = 2 * odd - 1
    outer, partner = lax.rem(gx + side + nx, nx), gx - side
    far_outer, far_partner = lax.rem(gx + 2 * side + nx, nx), lax.rem(gx - 2 * side + nx, nx)
    peers = (outer, partner, far_outer, far_partner) if FAR else (outer, partner)
    barrier = pltpu.get_barrier_semaphore()
    for peer in peers:
        pl.semaphore_signal(barrier, inc=1, device_id=(peer, gy), device_id_type=MESH)

    @pl.when(gy > 0)
    def _():
        pl.semaphore_signal(barrier, inc=1, device_id=(gx, gy - 1), device_id_type=MESH)

    @pl.when(gy < ny - 1)
    def _():
        pl.semaphore_signal(barrier, inc=1, device_id=(gx, gy + 1), device_id_type=MESH)

    low, high = jnp.minimum(gy, 1), jnp.minimum(ny - 1 - gy, 1)
    kind = low + 1 - high
    pltpu.make_async_copy(tables.at[kind], late.at[0:t_rows], load_sem.at[1]).start()
    pltpu.make_async_copy(stretch, late.at[t_rows : t_rows + ny], load_sem.at[1]).start()
    pltpu.make_async_copy(metric, late.at[t_rows + ny : t_rows + 2 * ny], load_sem.at[1]).start()

    place = lax.broadcasted_iota(jnp.int32, (8, width), 0)

    def powers(r, falling):
        tile = jnp.full((8, width), r ** (8 if falling else 1), jnp.float32)
        for n in range(1, 8):
            tile = jnp.where(place == n, np.float32(r ** (8 - n if falling else n + 1)), tile)
        return tile

    up1, down1 = powers(R1, False), powers(R1, True)
    up2, down2 = powers(R2, False), powers(R2, True)

    pltpu.make_async_copy(vel, f, load_sem.at[0]).wait()
    step1, step2 = np.float32(R1**8), np.float32(R2**8)

    def weighted(c, order, step, base):
        total = f[c, 8 * order[0] : 8 * order[0] + 8]
        for m in order[1:]:
            total = total * step + f[c, 8 * m : 8 * m + 8]
        return jnp.sum(total * base, axis=0, keepdims=True)

    rising, falling = list(range(steps)), list(range(steps))[::-1]
    to_right, to_left = 1 - odd, odd
    for c in range(comps):
        xs[to_right, c : c + 1] = weighted(c, rising, step1, down1)
        xs[to_right, 8 + c : 9 + c] = weighted(c, rising, step2, down2)
        xs[to_right, 16 + c : 17 + c] = f[c, rows - 1 : rows]
        xs[to_left, c : c + 1] = weighted(c, falling, step1, up1)
        xs[to_left, 8 + c : 9 + c] = weighted(c, falling, step2, up2)
        xs[to_left, 16 + c : 17 + c] = f[c, 0:1]

    pl.semaphore_wait(barrier, len(peers) + low + high)

    def send(src, dst, sem, peer):
        return pltpu.make_async_remote_copy(
            src_ref=src, dst_ref=dst, send_sem=sem.at[0], recv_sem=sem.at[1],
            device_id=peer, device_id_type=MESH,
        )

    send(xs.at[0], xr.at[0, 0:24], x_sem, (outer, gy)).start()
    if FAR:
        send(xs.at[1, 0:16], xr.at[0, 24:40], x_sem, (far_partner, gy)).start()
    send(xs.at[1], xr.at[1, 0:24], x_sem, (partner, gy)).start()
    if FAR:
        send(xs.at[0, 0:16], xr.at[1, 24:40], x_sem, (far_outer, gy)).start()

    pltpu.make_async_copy(late, late, load_sem.at[1]).wait()
    flat = f[...].reshape(comps * rows, width)
    ys[...] = lax.dot_general(
        late[0:8], flat, (((1,), (1,)), ((), ())), precision=HIGHEST,
        preferred_element_type=jnp.float32,
    )

    @pl.when(gy < ny - 1)
    def _():
        send(ys, yr.at[0:8], y_sem, (gx, gy + 1)).start()

    @pl.when(gy > 0)
    def _():
        send(ys, yr.at[8:16], y_sem, (gx, gy - 1)).start()

    @pl.when(gy == 0)
    def _():
        yr[0:8] = jnp.zeros((8, comps * rows), jnp.float32)

    @pl.when(gy == ny - 1)
    def _():
        yr[8:16] = jnp.zeros((8, comps * rows), jnp.float32)

    lanes = jnp.concatenate([f[c] for c in range(comps)], axis=1)
    own_x = jnp.dot(
        late[40 : 40 + 2 * rows][:, :rows], lanes, precision=HIGHEST,
        preferred_element_type=jnp.float32,
    )
    y_at = 40 + 2 * rows
    y_inner = jnp.concatenate([late[y_at + n * width : y_at + (n + 1) * width] for n in range(2)], axis=1)
    own_y = jnp.dot(flat, y_inner, precision=HIGHEST, preferred_element_type=jnp.float32)
    inv = 1.0 / late[pl.ds(t_rows + gy, 1), :]
    inv2 = inv * inv
    bend = -0.5 * late[pl.ds(t_rows + ny + gy, 1), :] * inv2 * inv

    def along_y(part, c):
        block = part[c * rows : (c + 1) * rows]
        v = f[3 * (c // 3) + 1]
        return block[:, :width] * (bend - v * inv) + block[:, width:] * inv2

    for c in range(comps):
        at = slice(c * width, (c + 1) * width)
        u = f[3 * (c // 3)]
        out[c] = own_x[rows:, at] - u * own_x[:rows, at] + along_y(own_y, c)

    inside = low + high == 2

    @pl.when(inside)
    def _():
        send(yr, yr, y_sem, (partner, gy)).wait_recv()

    @pl.when(jnp.logical_not(inside))
    def _():
        send(ys, ys, y_sem, (partner, gy)).wait_recv()

    spread = jnp.concatenate([late[8:24], late[24:40]], axis=1)
    beside = lax.dot_general(
        yr[...], spread, (((0,), (0,)), ((), ())), precision=HIGHEST,
        preferred_element_type=jnp.float32,
    )
    for c in range(comps):
        out[c] = out[c] + along_y(beside, c)

    send(xr, xr, x_sem, (partner, gy)).wait_recv()
    left, right = odd, 1 - odd
    far1, far2 = np.float32(R1**rows), np.float32(R2**rows)
    left1, left2 = xr[left, 0:8], xr[left, 8:16]
    right1, right2 = xr[right, 0:8], xr[right, 8:16]
    if FAR:
        left1, left2 = left1 + far1 * xr[left, 24:32], left2 + far2 * xr[left, 32:40]
        right1, right2 = right1 + far1 * xr[right, 24:32], right2 + far2 * xr[right, 32:40]
    left1, right1 = left1 * np.float32(G1 / R1), right1 * np.float32(-G1 / R1)
    left2, right2 = left2 * np.float32(0.5 * G2 / R2), right2 * np.float32(0.5 * G2 / R2)
    left_cell, right_cell = xr[left, 16:24], xr[right, 16:24]
    for c in range(comps):
        row = slice(c, c + 1)
        u = f[3 * (c // 3)]
        from_left1, from_right1 = up1 * left1[row], down1 * right1[row]
        from_left2, from_right2 = up2 * left2[row], down2 * right2[row]
        for m in range(steps):
            part = slice(8 * m, 8 * m + 8)
            lo, hi = np.float32(R1 ** (8 * m)), np.float32(R1 ** (rows - 8 - 8 * m))
            first = from_left1 * lo + from_right1 * hi
            lo, hi = np.float32(R2 ** (8 * m)), np.float32(R2 ** (rows - 8 - 8 * m))
            second = from_left2 * lo + from_right2 * hi
            if m == 0:
                cell = jnp.where(place == 0, left_cell[row], 0.0)
                first, second = first + NEAR1 * cell, second + 0.5 * NEAR2 * cell
            if m == steps - 1:
                cell = jnp.where(place == 7, right_cell[row], 0.0)
                first, second = first - NEAR1 * cell, second + 0.5 * NEAR2 * cell
            out[c, part] = out[c, part] + (second - u[part] * first)

    if FAR:
        send(xr, xr, x_sem, (partner, gy)).wait_send()
    else:
        send(xs, xs, x_sem, (partner, gy)).wait_send()

    @pl.when(inside)
    def _():
        send(yr, yr, y_sem, (partner, gy)).wait_send()

    @pl.when(jnp.logical_not(inside))
    def _():
        send(ys, ys, y_sem, (partner, gy)).wait_send()


def solution(mesh):
    nx, ny = mesh.shape["gx"], mesh.shape["gy"]

    def shards(velocity, stretch, second_metric):
        planes, parts, rows, width = velocity.shape
        comps = planes * parts
        x_inner = np.pad(x_tables(rows), ((0, 0), (0, width - rows)))
        y_inner, gather, spread = y_tables(ny * width, width)
        tables = np.stack(
            [
                np.concatenate(
                    [
                        gather, spread[:, :width], spread[:, width:], x_inner,
                        y_inner[q][:, :width], y_inner[q][:, width:],
                    ]
                )
                for q in (0, 1, ny - 1)
            ]
        )
        hbm = pl.BlockSpec(memory_space=pltpu.MemorySpace.HBM)
        f32 = jnp.float32
        out = pl.pallas_call(
            functools.partial(kernel, nx, ny),
            out_shape=pltpu.VMEM((comps, rows, width), f32),
            in_specs=[hbm] * 4,
            out_specs=pl.BlockSpec(memory_space=pltpu.VMEM),
            scratch_shapes=[
                pltpu.VMEM((comps, rows, width), f32),
                pltpu.VMEM((tables.shape[1] + 2 * ny, width), f32),
                pltpu.VMEM((2, 24, width), f32),
                pltpu.VMEM((8, comps * rows), f32),
                pltpu.VMEM((2, 40 if FAR else 24, width), f32),
                pltpu.VMEM((16, comps * rows), f32),
                pltpu.SemaphoreType.DMA((2,)),
                pltpu.SemaphoreType.DMA((2,)),
                pltpu.SemaphoreType.DMA((2,)),
            ],
            compiler_params=pltpu.CompilerParams(collective_id=0, has_side_effects=True),
        )(
            velocity.reshape(comps, rows, width), jnp.asarray(tables),
            stretch.reshape(ny, width), second_metric.reshape(ny, width),
        )
        return out.reshape(velocity.shape)

    return jax.shard_map(
        shards,
        mesh=mesh,
        in_specs=(P(None, None, "gx", "gy"), P(), P()),
        out_specs=P(None, None, "gx", "gy"),
        check_vma=False,
    )
```

```python
import functools

import jax
import jax.numpy as jnp
import numpy as np
from jax import lax
from jax.experimental import pallas as pl
from jax.experimental.pallas import tpu as pltpu
from jax.sharding import PartitionSpec as P

MESH = pl.DeviceIdType.MESH
HIGHEST = lax.Precision.HIGHEST

C1, C2 = 1.0 / 3.0, 2.0 / 11.0
R1 = (-1.0 + np.sqrt(1.0 - 4.0 * C1 * C1)) / (2.0 * C1)
R2 = (-1.0 + np.sqrt(1.0 - 4.0 * C2 * C2)) / (2.0 * C2)
K1 = 1.0 / (1.0 + 2.0 * C1 * R1)
K2 = 1.0 / (1.0 + 2.0 * C2 * R2)
G1 = (25.0 / 36.0) * K1 * (R1 - 1.0 / R1)
G2 = -(75.0 / 88.0) * 7.5 * K2
NEAR1 = -1.0 / 12.0
NEAR2 = 3.0 / 8.0
ZERO2 = (75.0 / 88.0) * (5.5 - 7.5 * K2) - 0.75


def x_tables(rows):
    d = np.arange(rows)[:, None] - np.arange(rows)[None, :]
    first = G1 * np.sign(d) * R1 ** np.abs(d) + NEAR1 * np.where(np.abs(d) == 1, np.sign(d), 0)
    second = G2 * R2 ** np.abs(d) * (d != 0) + NEAR2 * (np.abs(d) == 1) + ZERO2 * (d == 0)
    inner = np.concatenate([first, 0.5 * second])
    return inner.astype(np.float32)


def y_tables(total, width):
    rows = np.arange(total)
    near = (rows == 1) | (rows == total - 2)
    edge = (rows == 0) | (rows == total - 1)
    bands = (
        np.where(edge, 0.0, np.where(near, 0.25, C1)),
        np.where(edge, 0.0, np.where(near, 0.1, C2)),
    )
    b1 = np.zeros((total, total))
    b2 = np.zeros((total, total))
    for j in range(2, total - 2):
        b1[j, j - 2 : j + 3] = [-1 / 36, -7 / 9, 0.0, 7 / 9, 1 / 36]
        b2[j, j - 2 : j + 3] = [3 / 44, 12 / 11, -24 / 11 - 6 / 44, 12 / 11, 3 / 44]
    for j in (1, total - 2):
        b1[j, j - 1 : j + 2] = [-0.75, 0.0, 0.75]
        b2[j, j - 1 : j + 2] = [1.2, -2.4, 1.2]
    b1[0, :3] = [-1.5, 2.0, -0.5]
    b1[-1, -3:] = [0.5, -2.0, 1.5]
    b2[0, :4] = [2.0, -5.0, 4.0, -1.0]
    b2[-1, -4:] = [-1.0, 4.0, -5.0, 2.0]
    whole = []
    for band, b in zip(bands, (b1, b2)):
        a = np.eye(total) + np.diag(band[1:], -1) + np.diag(band[:-1], 1)
        whole.append(np.linalg.solve(a, b))
    blocks = total // width
    inner = np.zeros((blocks, width, 2 * width))
    for q in range(blocks):
        own = slice(q * width, (q + 1) * width)
        inner[q, :, :width] = whole[0][own, own].T
        inner[q, :, width:] = 0.5 * whole[1][own, own].T
    up = np.arange(1, width + 1)
    down = width - np.arange(width)
    gather = np.zeros((8, width))
    gather[0], gather[1], gather[2, -1] = R1**down, R2**down, 1.0
    gather[3], gather[4], gather[5, 0] = R1**up, R2**up, 1.0
    spread = np.zeros((16, 2 * width))
    spread[0, :width] = G1 * R1 ** (up - 1)
    spread[1, width:] = 0.5 * G2 * R2 ** (up - 1)
    spread[2, 0], spread[2, width] = NEAR1, 0.5 * NEAR2
    spread[11, :width] = -G1 * R1 ** (down - 1)
    spread[12, width:] = 0.5 * G2 * R2 ** (down - 1)
    spread[13, width - 1], spread[13, 2 * width - 1] = -NEAR1, 0.5 * NEAR2
    small = np.finfo(np.float32).tiny
    return [
        np.where(np.abs(t) < small, 0.0, t).astype(np.float32)
        for t in (inner, gather, spread)
    ]


def kernel(
    nx, ny, vel, tables, stretch, metric, out, f, late, xs, ys, xr, yr,
    sems, ready,
):
    gx = lax.axis_index("gx")
    gy = lax.axis_index("gy")
    comps, rows, width = f.shape
    steps = rows // 8
    t_rows = tables.shape[1]

    def row_copy(n):
        part = slice(n * comps // 3, (n + 1) * comps // 3)
        return pltpu.make_async_copy(vel.at[part], f.at[part], sems.at[0])

    for n in range(3):
        row_copy(n).start()

    last = nx - 1
    barrier = pltpu.get_barrier_semaphore()

    def tell(sem, cond, x, y):
        @pl.when(cond)
        def _():
            pl.semaphore_signal(sem, inc=1, device_id=(x, y), device_id_type=MESH)

    right, left = lax.rem(gx + 1, nx), lax.rem(gx + last, nx)
    right2, left2 = lax.rem(gx + 2, nx), lax.rem(gx + last - 1, nx)
    tell(barrier, gx < last, right, gy)
    tell(barrier, gx < last - 1, right2, gy)
    pl.semaphore_signal(barrier, inc=1, device_id=(left, gy), device_id_type=MESH)
    pl.semaphore_signal(barrier, inc=1, device_id=(left2, gy), device_id_type=MESH)
    tell(barrier, gy < ny - 1, gx, gy + 1)

    low, high = jnp.minimum(gy, 1), jnp.minimum(ny - 1 - gy, 1)
    kind = low + 1 - high
    pltpu.make_async_copy(tables.at[kind], late.at[0:t_rows], sems.at[1]).start()
    pltpu.make_async_copy(stretch, late.at[t_rows : t_rows + ny], sems.at[1]).start()
    pltpu.make_async_copy(metric, late.at[t_rows + ny : t_rows + 2 * ny], sems.at[1]).start()

    place = lax.broadcasted_iota(jnp.int32, (8, width), 0)

    def powers(r, falling):
        tile = jnp.full((8, width), r ** (8 if falling else 1), jnp.float32)
        for n in range(1, 8):
            tile = jnp.where(place == n, np.float32(r ** (8 - n if falling else n + 1)), tile)
        return tile

    up1, down1 = powers(R1, False), powers(R1, True)
    up2, down2 = powers(R2, False), powers(R2, True)

    pltpu.make_async_copy(vel, f, sems.at[0]).wait()
    step1, step2 = np.float32(R1**8), np.float32(R2**8)

    def weighted(c, order, step, base):
        total = f[c, 8 * order[0] : 8 * order[0] + 8]
        for m in order[1:]:
            total = total * step + f[c, 8 * m : 8 * m + 8]
        return jnp.sum(total * base, axis=0, keepdims=True)

    rising, falling = list(range(steps)), list(range(steps))[::-1]
    to_right, to_left = 0, 1
    for c in range(comps):
        xs[to_right, c : c + 1] = weighted(c, rising, step1, down1)
        xs[to_right, 8 + c : 9 + c] = weighted(c, rising, step2, down2)
        xs[to_right, 16 + c : 17 + c] = f[c, rows - 1 : rows]
        xs[to_left, c : c + 1] = weighted(c, falling, step1, up1)
        xs[to_left, 8 + c : 9 + c] = weighted(c, falling, step2, up2)
        xs[to_left, 16 + c : 17 + c] = f[c, 0:1]

    def flag(value):
        return jnp.minimum(jnp.maximum(value, 0), 1)

    pl.semaphore_wait(barrier, 2 + flag(gx) + flag(gx - 1) + low)

    def send(src, dst, pair, peer):
        return pltpu.make_async_remote_copy(
            src_ref=src, dst_ref=dst, send_sem=sems.at[pair], recv_sem=sems.at[pair + 1],
            device_id=peer, device_id_type=MESH,
        )

    def send_left():
        send(xs.at[1], xr.at[1, 0:24], 2, (left, gy)).start()

    def send_left2():
        send(xs.at[1, 0:16], xr.at[1, 24:40], 2, (left2, gy)).start()

    send(xs.at[0], xr.at[0, 0:24], 2, (right, gy)).start()
    pl.when(gx > 0)(send_left)
    send(xs.at[0, 0:16], xr.at[0, 24:40], 2, (right2, gy)).start()
    pl.when(gx > 1)(send_left2)
    tell(ready.at[0], gx == last, 0, gy)
    tell(ready.at[0], gx == last, 1, gy)
    tell(ready.at[0], gx == last - 1, 0, gy)
    tell(ready.at[1], gy > 0, gx, gy - 1)

    pltpu.make_async_copy(late, late, sems.at[1]).wait()
    flat = f[...].reshape(comps * rows, width)
    ys[...] = lax.dot_general(
        late[0:8], flat, (((1,), (1,)), ((), ())), precision=HIGHEST,
        preferred_element_type=jnp.float32,
    )

    @pl.when(gy > 0)
    def _():
        send(ys, yr.at[8:16], 4, (gx, gy - 1)).start()

    @pl.when(gy == 0)
    def _():
        yr[0:8] = jnp.zeros((8, comps * rows), jnp.float32)

    @pl.when(gy == ny - 1)
    def _():
        yr[8:16] = jnp.zeros((8, comps * rows), jnp.float32)

    lanes = jnp.concatenate([f[c] for c in range(comps)], axis=1)
    own_x = jnp.dot(
        late[40 : 40 + 2 * rows][:, :rows], lanes, precision=HIGHEST,
        preferred_element_type=jnp.float32,
    )
    y_at = 40 + 2 * rows
    y_inner = jnp.concatenate([late[y_at + n * width : y_at + (n + 1) * width] for n in range(2)], axis=1)
    own_y = jnp.dot(flat, y_inner, precision=HIGHEST, preferred_element_type=jnp.float32)
    inv = 1.0 / late[pl.ds(t_rows + gy, 1), :]
    inv2 = inv * inv
    bend = -0.5 * late[pl.ds(t_rows + ny + gy, 1), :] * inv2 * inv

    def along_y(part, c):
        block = part[c * rows : (c + 1) * rows]
        v = f[3 * (c // 3) + 1]
        return block[:, :width] * (bend - v * inv) + block[:, width:] * inv2

    for c in range(comps):
        at = slice(c * width, (c + 1) * width)
        u = f[3 * (c // 3)]
        out[c] = own_x[rows:, at] - u * own_x[:rows, at] + along_y(own_y, c)

    @pl.when(gy < ny - 1)
    def _():
        pl.semaphore_wait(ready.at[1], 1)
        send(ys, yr.at[0:8], 4, (gx, gy + 1)).start()

    @pl.when(gx < 2)
    def _():
        pl.semaphore_wait(ready.at[0], 2 - gx)
        send_left2()

    pl.when(gx == 0)(send_left)

    inside = low + high == 2

    @pl.when(inside)
    def _():
        send(yr, yr, 4, (right, gy)).wait_recv()

    @pl.when(jnp.logical_not(inside))
    def _():
        send(ys, ys, 4, (right, gy)).wait_recv()

    spread = jnp.concatenate([late[8:24], late[24:40]], axis=1)
    beside = lax.dot_general(
        yr[...], spread, (((0,), (0,)), ((), ())), precision=HIGHEST,
        preferred_element_type=jnp.float32,
    )
    for c in range(comps):
        out[c] = out[c] + along_y(beside, c)

    send(xr, xr, 2, (right, gy)).wait_recv()
    far1, far2 = np.float32(R1**rows), np.float32(R2**rows)
    left1, left2 = xr[0, 0:8], xr[0, 8:16]
    right1, right2 = xr[1, 0:8], xr[1, 8:16]
    left1, left2 = left1 + far1 * xr[0, 24:32], left2 + far2 * xr[0, 32:40]
    right1, right2 = right1 + far1 * xr[1, 24:32], right2 + far2 * xr[1, 32:40]
    left1, right1 = left1 * np.float32(G1 / R1), right1 * np.float32(-G1 / R1)
    left2, right2 = left2 * np.float32(0.5 * G2 / R2), right2 * np.float32(0.5 * G2 / R2)
    left_cell, right_cell = xr[0, 16:24], xr[1, 16:24]
    for c in range(comps):
        row = slice(c, c + 1)
        u = f[3 * (c // 3)]
        from_left1, from_right1 = up1 * left1[row], down1 * right1[row]
        from_left2, from_right2 = up2 * left2[row], down2 * right2[row]
        for m in range(steps):
            part = slice(8 * m, 8 * m + 8)
            lo, hi = np.float32(R1 ** (8 * m)), np.float32(R1 ** (rows - 8 - 8 * m))
            first = from_left1 * lo + from_right1 * hi
            lo, hi = np.float32(R2 ** (8 * m)), np.float32(R2 ** (rows - 8 - 8 * m))
            second = from_left2 * lo + from_right2 * hi
            if m == 0:
                cell = jnp.where(place == 0, left_cell[row], 0.0)
                first, second = first + NEAR1 * cell, second + 0.5 * NEAR2 * cell
            if m == steps - 1:
                cell = jnp.where(place == 7, right_cell[row], 0.0)
                first, second = first - NEAR1 * cell, second + 0.5 * NEAR2 * cell
            out[c, part] = out[c, part] + (second - u[part] * first)

    send(xr, xr, 2, (right, gy)).wait_send()

    @pl.when(inside)
    def _():
        send(yr, yr, 4, (right, gy)).wait_send()

    @pl.when(jnp.logical_not(inside))
    def _():
        send(ys, ys, 4, (right, gy)).wait_send()


def solution(mesh):
    nx, ny = mesh.shape["gx"], mesh.shape["gy"]

    def shards(velocity, stretch, second_metric):
        planes, parts, rows, width = velocity.shape
        comps = planes * parts
        x_inner = np.pad(x_tables(rows), ((0, 0), (0, width - rows)))
        y_inner, gather, spread = y_tables(ny * width, width)
        tables = np.stack(
            [
                np.concatenate(
                    [
                        gather, spread[:, :width], spread[:, width:], x_inner,
                        y_inner[q][:, :width], y_inner[q][:, width:],
                    ]
                )
                for q in (0, 1, ny - 1)
            ]
        )
        hbm = pl.BlockSpec(memory_space=pltpu.MemorySpace.HBM)
        f32 = jnp.float32
        out = pl.pallas_call(
            functools.partial(kernel, nx, ny),
            out_shape=pltpu.VMEM((comps, rows, width), f32),
            in_specs=[hbm] * 4,
            out_specs=pl.BlockSpec(memory_space=pltpu.VMEM),
            scratch_shapes=[
                pltpu.VMEM((comps, rows, width), f32),
                pltpu.VMEM((tables.shape[1] + 2 * ny, width), f32),
                pltpu.VMEM((2, 24, width), f32),
                pltpu.VMEM((8, comps * rows), f32),
                pltpu.VMEM((2, 40, width), f32),
                pltpu.VMEM((16, comps * rows), f32),
                pltpu.SemaphoreType.DMA((6,)),
                pltpu.SemaphoreType.REGULAR((2,)),
            ],
            compiler_params=pltpu.CompilerParams(collective_id=0, has_side_effects=True),
        )(
            velocity.reshape(comps, rows, width), jnp.asarray(tables),
            stretch.reshape(ny, width), second_metric.reshape(ny, width),
        )
        return out.reshape(velocity.shape)

    return jax.shard_map(
        shards,
        mesh=mesh,
        in_specs=(P(None, None, "gx", "gy"), P(), P()),
        out_specs=P(None, None, "gx", "gy"),
        check_vma=False,
    )
```
